512 devices in a mesh: band: 8 (over z_hi, core), gx: 8 (over x, z_lo), gy: 8 (over y).
Axes of the slice: x: 4, y: 8, z: 8 (z_hi: 4, z_lo: 2; z = z_hi * 2 + z_lo), core: 2. Of those that a mesh axis runs over, the one named last changes fastest.
Arguments:
- start_bands: float32 [64, 48, 64, 128], P('band', 'gx', 'gy'), may hold values from -40 to 40
- potential: float32 [48, 64, 128], P('gx', 'gy'), may hold values from 0 to 2
Outputs:
- new_bands: float32 [64, 48, 64, 128], P('band', 'gx', 'gy')
The draws below stay inside these ranges and needn't reach their ends.
All inputs are finite; a program needn't handle non-finite values.
Results may differ from the reference program's by a relative error of at most 0.00025.
Values sent between devices are 32-bit elements; how exact they have to be, the bound alone decides.
A program may use at most 64 MiB of HBM per device.

```python
import math
import jax
import jax.numpy as jnp
from jax import lax

BANDS = 64
NZ = 128
DEGREE = 4
NX = 48
NY = 64


def draw_start_bands(key, part):
    first_key, second_key = jax.random.split(key, 2)
    column_scale = jnp.exp(jax.random.uniform(second_key, (1, NX, NY, 1), jnp.float32) * math.log(10.0))
    values = jax.random.normal(first_key, (BANDS, NX, NY, NZ), jnp.float32) * column_scale
    return jnp.clip(values, -40.0, 40.0).astype(jnp.float32)


def steps_of(key, dims, shards, smallest, top_value):
    def one(axis_at, parts):
        heights = jax.random.uniform(jax.random.fold_in(jax.random.fold_in(key, 6), axis_at), (parts,), jnp.float32, smallest / len(shards), top_value / len(shards))
        return jnp.repeat(jnp.exp(heights), dims[axis_at] // parts).reshape((-1,) + (1,) * (len(dims) - axis_at - 1))

    gain = one(*shards[0])
    for cut in shards[1:]:
        gain = gain * one(*cut)
    return gain


def setup_inputs(seed: int = 0) -> dict:
    streams_of = jax.random.split(jax.random.key(seed), 3)
    return {
        "start_bands": draw_start_bands(jax.random.fold_in(streams_of[2], 71), 0),
        "potential": jnp.clip(2.0 * jax.random.uniform(streams_of[1], (NX, NY, NZ), jnp.float32) ** steps_of(streams_of[1], (NX, NY, NZ), ((0, 8), (1, 8)), -0.2, 0.2), 0.0, 2.0),
    }


COEFFS = (-5369.0 / 1800.0, 12.0 / 7.0, -15.0 / 56.0, 10.0 / 189.0, -1.0 / 112.0, 2.0 / 1925.0, -1.0 / 16632.0)
LOWER_END = -0.5
CUT_LOW = 3.0
CUT_HIGH = 12.7

def filter_weights(degree):
    half_width = (CUT_HIGH - CUT_LOW) / 2.0
    middle = (CUT_HIGH + CUT_LOW) / 2.0
    sigma = half_width / (LOWER_END - middle)
    tau = 2.0 / sigma
    first = sigma / half_width
    others = []
    for index in range(degree - 1):
        sigma_new = 1.0 / (tau - sigma)
        others.append((2.0 * sigma_new / half_width, sigma * sigma_new))
        sigma = sigma_new
    return (middle, first, others)

def hamiltonian(field, potential):
    laplace = 3.0 * COEFFS[0] * field
    for offset in range(1, len(COEFFS)):
        neighbours = jnp.roll(field, -offset, 0) + jnp.roll(field, offset, 0)
        neighbours = neighbours + jnp.roll(field, -offset, 1) + jnp.roll(field, offset, 1)
        neighbours = neighbours + jnp.roll(field, -offset, 2) + jnp.roll(field, offset, 2)
        laplace = laplace + COEFFS[offset] * neighbours
    return -0.5 * laplace + potential * field

def filter_band(field, potential):
    middle, first, others = filter_weights(DEGREE)
    current = (hamiltonian(field, potential) - middle * field) * first
    previous = field
    for scale_now, scale_back in others:
        following = (hamiltonian(current, potential) - middle * current) * scale_now - scale_back * previous
        previous = current
        current = following
    return current

def reference(start_bands, potential):
    filtered = lax.map(lambda field: filter_band(field, potential), start_bands)
    flattened = filtered.reshape(filtered.shape[0], -1)
    margin = jnp.dot(flattened.astype(jnp.float32), flattened.T.astype(jnp.float32), precision=lax.Precision.HIGHEST, preferred_element_type=jnp.float32) * (1.0 / (NX * NY * NZ))
    lower_factor = jnp.linalg.cholesky(margin)
    identity = jnp.eye(margin.shape[0], dtype=jnp.float32)
    inverse = jax.scipy.linalg.solve_triangular(lower_factor, identity, lower=True)
    rotated = jnp.dot(inverse.astype(jnp.float32), flattened.astype(jnp.float32), precision=lax.Precision.HIGHEST, preferred_element_type=jnp.float32)
    return rotated.reshape(start_bands.shape)
```

```python
import jax
import jax.numpy as jnp
from jax import lax
from jax.experimental import pallas as pl
from jax.experimental.pallas import tpu as pltpu
from jax.sharding import PartitionSpec as P

DEGREE = 4
COEFFS = (
    -5369.0 / 1800.0,
    12.0 / 7.0,
    -15.0 / 56.0,
    10.0 / 189.0,
    -1.0 / 112.0,
    2.0 / 1925.0,
    -1.0 / 16632.0,
)
LOWER_END = -0.5
CUT_LOW = 3.0
CUT_HIGH = 12.7
REACH = 6
MESH = pl.DeviceIdType.MESH
NB, NG, NY = 8, 8, 8
XW, YW, NX, NZ = 6, 8, 48, 128
BANDS = 64
CELLS = 48 * 64 * 128


def filter_weights(degree):
    half_width = (CUT_HIGH - CUT_LOW) / 2.0
    middle = (CUT_HIGH + CUT_LOW) / 2.0
    sigma = half_width / (LOWER_END - middle)
    tau = 2.0 / sigma
    first = sigma / half_width
    others = []
    for index in range(degree - 1):
        sigma_new = 1.0 / (tau - sigma)
        others.append((2.0 * sigma_new / half_width, sigma * sigma_new))
        sigma = sigma_new
    return (middle, first, others)


def wait_bytes(ref, sem):
    pltpu.make_async_copy(ref, ref, sem).wait()


def dot(a, b, contract):
    return lax.dot_general(
        a,
        b,
        (contract, ((), ())),
        precision=lax.Precision.HIGHEST,
        preferred_element_type=jnp.float32,
    )


def inverse_factor(packed):
    lane = lax.broadcasted_iota(jnp.int32, (8, 128), 1)
    sub = lax.broadcasted_iota(jnp.int32, (8, 128), 0)
    rows = []
    for t in range(8):
        part = packed[8 * (t % 4) : 8 * (t % 4) + 8]
        if t >= 4:
            part = pltpu.roll(part, 64, 1)
        unit = jnp.where(lane == sub + 8 * t, 1.0, 0.0)
        rows.append(jnp.where(lane >= 64, part, unit))
    for k in range(BANDS - 1):
        t, s = divmod(k, 8)
        row = jnp.broadcast_to(rows[t][s : s + 1, :], (8, 128))
        pivot = jnp.broadcast_to(rows[t][s : s + 1, 64 + k : 65 + k], (8, 128))
        scaled = row / pivot
        for i in range(t, 8):
            column = jnp.broadcast_to(rows[i][:, 64 + k : 65 + k], (8, 128))
            if i == t:
                column = jnp.where(sub > s, column, 0.0)
            rows[i] = rows[i] - column * scaled
    done = []
    for t in range(8):
        pivots = jnp.sum(jnp.where(lane == sub + (8 * t + 64), rows[t], 0.0), axis=1, keepdims=True)
        done.append(rows[t] * (1.0 / jnp.sqrt(pivots)))
    return jnp.concatenate(done, axis=0)[:, :BANDS]


def kernel(
    start,
    pot,
    out,
    own,
    own_pot,
    field,
    last,
    pots,
    acc,
    pencil,
    rotated,
    packed,
    half,
    both,
    sum_y,
    sum_z,
    sum_x,
    local_sem,
    ax_send,
    ax_recv,
    pot_send,
    pot_recv,
    first_send,
    first_recv,
    halo_send,
    halo_recv,
    pen_send,
    pen_recv,
    sum_send,
    sum_recv,
    back_send,
    back_recv,
):
    b = lax.axis_index("band")
    g = lax.axis_index("gx")
    r = lax.axis_index("gy")

    def remote(src, dst, send, recv, device):
        copy = pltpu.make_async_remote_copy(
            src_ref=src, dst_ref=dst, send_sem=send, recv_sem=recv, device_id=device, device_id_type=MESH
        )
        copy.start()
        return copy

    load = pltpu.make_async_copy(start, own, local_sem.at[0])
    load.start()
    load_pot = pltpu.make_async_copy(pot, own_pot, local_sem.at[1])
    load_pot.start()

    plane_peers = [(db, dg) for db in range(NB) for dg in range(NG) if db or dg]
    barrier = pltpu.get_barrier_semaphore()
    for db, dg in plane_peers:
        device = {"band": lax.rem(b + db, NB), "gx": lax.rem(g + dg, NG)}
        pl.semaphore_signal(barrier, inc=1, device_id=device, device_id_type=MESH)
    for dy in range(1, NY):
        pl.semaphore_signal(barrier, inc=1, device_id={"gy": lax.rem(r + dy, NY)}, device_id_type=MESH)
    pl.semaphore_wait(barrier, len(plane_peers) + NY - 1)
    load.wait()
    load_pot.wait()

    for dg in range(1, NG):
        to = lax.rem(g + dg, NG)
        for x in range(XW):
            remote(
                own.at[to, x],
                field.at[0, pl.ds(REACH, YW), XW * g + x, :],
                ax_send,
                ax_recv.at[g],
                {"gx": to},
            )
    mine = []
    for x in range(XW):
        copy = pltpu.make_async_copy(
            own.at[g, x], field.at[0, pl.ds(REACH, YW), XW * g + x, :], local_sem.at[2 + x]
        )
        copy.start()
        mine.append(copy)
    for copy in mine:
        copy.wait()

    up = {"gy": lax.rem(r + 1, NY)}
    down = {"gy": lax.rem(r + NY - 1, NY)}

    def forward(index):
        cols = pl.ds(XW * index, XW)
        remote(
            field.at[0, pl.ds(YW, REACH), cols, :],
            field.at[0, pl.ds(0, REACH), cols, :],
            first_send.at[0],
            first_recv.at[0],
            up,
        )
        remote(
            field.at[0, pl.ds(REACH, REACH), cols, :],
            field.at[0, pl.ds(YW + REACH, REACH), cols, :],
            first_send.at[1],
            first_recv.at[1],
            down,
        )

    forward(g)
    for dg in range(1, NG):
        source = lax.rem(g + NG - dg, NG)
        wait_bytes(field.at[0, pl.ds(REACH, YW), pl.ds(XW * source, XW), :], ax_recv.at[source])
        forward(source)
    wait_bytes(own.at[pl.ds(0, NG - 1)], ax_send)

    for dg in range(1, NG):
        to = lax.rem(g + dg, NG)
        for x in range(XW):
            remote(own_pot.at[x], pots.at[:, XW * g + x, :], pot_send, pot_recv, {"gx": to})
    mine = []
    for x in range(XW):
        copy = pltpu.make_async_copy(own_pot.at[x], pots.at[:, XW * g + x, :], local_sem.at[2 + x])
        copy.start()
        mine.append(copy)
    for copy in mine:
        copy.wait()
    wait_bytes(pots.at[:, pl.ds(0, XW * (NG - 1)), :], pot_recv)
    wait_bytes(pots.at[:, pl.ds(0, XW * (NG - 1)), :], pot_send)

    middle, first, others = filter_weights(DEGREE)
    for k in range(DEGREE):
        scale = first if k == 0 else others[k - 1][0]
        weights = [-0.5 * c * scale for c in COEFFS]
        if k:
            moves = [
                remote(
                    field.at[k, pl.ds(YW, REACH)],
                    field.at[k, pl.ds(0, REACH)],
                    halo_send.at[k, 0],
                    halo_recv.at[k, 0],
                    up,
                ),
                remote(
                    field.at[k, pl.ds(REACH, REACH)],
                    field.at[k, pl.ds(YW + REACH, REACH)],
                    halo_send.at[k, 1],
                    halo_recv.at[k, 1],
                    down,
                ),
            ]

        def local_part(y, carry, k=k, scale=scale, weights=weights):
            plane = field[k, REACH + y]
            total = (scale * pots[y] + (3.0 * weights[0] - middle * scale)) * plane
            for j in range(1, REACH + 1):
                near = pltpu.roll(plane, j, 0) + pltpu.roll(plane, NX - j, 0)
                near = near + pltpu.roll(plane, j, 1) + pltpu.roll(plane, NZ - j, 1)
                total = total + weights[j] * near
            if k:
                total = total - others[k - 1][1] * field[k - 1, REACH + y]
            acc[y] = total
            return carry

        lax.fori_loop(0, YW, local_part, 0)
        for y in range(YW):
            total = acc[y]
            for j in range(1, REACH + 1):
                if y - j >= 0:
                    total = total + weights[j] * field[k, REACH + y - j]
                if y + j < YW:
                    total = total + weights[j] * field[k, REACH + y + j]
            acc[y] = total

        if k:
            for move in moves:
                move.wait()
        else:
            for side in range(2):
                low = 0 if side == 0 else YW + REACH
                wait_bytes(field.at[0, pl.ds(low, REACH)], first_recv.at[side])
                wait_bytes(field.at[0, pl.ds(low, REACH)], first_send.at[side])
        for y in range(YW):
            total = acc[y]
            for j in range(1, REACH + 1):
                if y - j < 0:
                    total = total + weights[j] * field[k, REACH + y - j]
                if y + j >= YW:
                    total = total + weights[j] * field[k, REACH + y + j]
            if k < DEGREE - 1:
                field[k + 1, REACH + y] = total
            else:
                last[y] = total

    band = NG * b + g
    for db, dg in plane_peers:
        to_b = lax.rem(b + db, NB)
        to_g = lax.rem(g + dg, NG)
        remote(
            last.at[to_b, pl.ds(XW * to_g, XW), :],
            pencil.at[:, band, :],
            pen_send,
            pen_recv,
            {"band": to_b, "gx": to_g},
        )
    copy = pltpu.make_async_copy(last.at[b, pl.ds(XW * g, XW), :], pencil.at[:, band, :], local_sem.at[0])
    copy.start()
    copy.wait()
    wait_bytes(pencil.at[:, pl.ds(0, BANDS - 1), :], pen_recv)
    wait_bytes(pencil.at[:, pl.ds(0, BANDS - 1), :], pen_send)

    cells = jnp.concatenate([pencil[x] for x in range(XW)], axis=1)
    twice = jnp.concatenate([cells, cells], axis=0)
    products = dot(cells, twice, ((1,), (1,)))
    lane = lax.broadcasted_iota(jnp.int32, (32, 128), 1)
    joined = jnp.where(lane < 64, products[32:], products[:32])
    packed[...] = joined.reshape(2, 16, 128)

    core = lax.rem(b, 2)
    partner = {"band": b + 1 - 2 * core}
    move = remote(packed.at[1 - core], half, sum_send.at[0], sum_recv.at[0], partner)
    move.wait()
    zhi, zlo, chip_x = b // 2, lax.rem(g, 2), g // 2

    def exchange(table, value, slot, peers, stage):
        table[slot] = value
        for device in peers:
            remote(table.at[slot], table.at[slot], sum_send.at[stage], sum_recv.at[stage], device)
        count = len(peers)
        wait_bytes(table.at[pl.ds(0, count)], sum_recv.at[stage])
        wait_bytes(table.at[pl.ds(0, count)], sum_send.at[stage])
        total = table[0]
        for i in range(1, count + 1):
            total = total + table[i]
        return total

    value = packed[core] + half[...]
    value = exchange(sum_y, value, r, [{"gy": lax.rem(r + d, NY)} for d in range(1, NY)], 1)
    place = 2 * zhi + zlo
    peers = []
    for d in range(1, 8):
        other = lax.rem(place + d, 8)
        peers.append({"band": 2 * (other // 2) + core, "gx": 2 * chip_x + lax.rem(other, 2)})
    value = exchange(sum_z, value, place, peers, 2)
    peers = [{"gx": 2 * lax.rem(chip_x + d, 4) + zlo} for d in range(1, 4)]
    value = exchange(sum_x, value, chip_x, peers, 3)
    both[core] = value * (1.0 / CELLS)
    move = remote(both.at[core], both.at[core], sum_send.at[4], sum_recv.at[4], partner)
    move.wait()

    inverse = inverse_factor(both[...].reshape(32, 128))
    for x in range(XW):
        rotated[x] = dot(inverse, pencil[x], ((1,), (0,)))

    for db in range(1, NB):
        to = lax.rem(b + db, NB)
        for x in range(XW):
            remote(
                rotated.at[x, pl.ds(8 * to, 8), :], out.at[:, x, b, :], back_send, back_recv, {"band": to}
            )
    mine = []
    for x in range(XW):
        copy = pltpu.make_async_copy(rotated.at[x, pl.ds(8 * b, 8), :], out.at[:, x, b, :], local_sem.at[2 + x])
        copy.start()
        mine.append(copy)
    for copy in mine:
        copy.wait()
    wait_bytes(own.at[pl.ds(0, NB - 1)], back_recv)
    wait_bytes(own.at[pl.ds(0, NB - 1)], back_send)


def on_device(start_bands, potential):
    f32 = jnp.float32
    dma = pltpu.SemaphoreType.DMA
    return pl.pallas_call(
        kernel,
        out_shape=jax.ShapeDtypeStruct((8, XW, YW, NZ), f32),
        in_specs=[pl.BlockSpec(memory_space=pl.ANY)] * 2,
        out_specs=pl.BlockSpec(memory_space=pl.ANY),
        scratch_shapes=[
            pltpu.VMEM((8, XW, YW, NZ), f32),
            pltpu.VMEM((XW, YW, NZ), f32),
            pltpu.VMEM((DEGREE, YW + 2 * REACH, NX, NZ), f32),
            pltpu.VMEM((YW, NX, NZ), f32),
            pltpu.VMEM((YW, NX, NZ), f32),
            pltpu.VMEM((YW, NX, NZ), f32),
            pltpu.VMEM((XW, BANDS, NZ), f32),
            pltpu.VMEM((XW, BANDS, NZ), f32),
            pltpu.VMEM((2, 16, 128), f32),
            pltpu.VMEM((16, 128), f32),
            pltpu.VMEM((2, 16, 128), f32),
            pltpu.VMEM((8, 16, 128), f32),
            pltpu.VMEM((8, 16, 128), f32),
            pltpu.VMEM((4, 16, 128), f32),
            dma((8,)),
            dma,
            dma((NG,)),
            dma,
            dma,
            dma((2,)),
            dma((2,)),
            dma((DEGREE, 2)),
            dma((DEGREE, 2)),
            dma,
            dma,
            dma((5,)),
            dma((5,)),
            dma,
            dma,
        ],
        compiler_params=pltpu.CompilerParams(collective_id=0, has_side_effects=True),
    )(start_bands, potential)


def solution(mesh):
    in_specs = (P("band", "gx", "gy", None), P("gx", "gy", None))
    out_specs = P("band", "gx", "gy", None)
    return jax.shard_map(on_device, mesh=mesh, in_specs=in_specs, out_specs=out_specs, check_vma=False)
```

```python
import jax
import jax.numpy as jnp
from jax import lax
from jax.experimental import pallas as pl
from jax.experimental.pallas import tpu as pltpu
from jax.sharding import PartitionSpec as P

DEGREE = 4
COEFFS = (
    -5369.0 / 1800.0,
    12.0 / 7.0,
    -15.0 / 56.0,
    10.0 / 189.0,
    -1.0 / 112.0,
    2.0 / 1925.0,
    -1.0 / 16632.0,
)
LOWER_END = -0.5
CUT_LOW = 3.0
CUT_HIGH = 12.7
REACH = 6
MESH = pl.DeviceIdType.MESH
NB, NG, NY = 8, 8, 8
XW, YW, NX, NZ = 6, 8, 48, 128
BANDS = 64
CELLS = 48 * 64 * 128
CHUNKS = 3
PIECES = {2: (0, 4, 8), 3: (0, 3, 6, 8)}[CHUNKS]
GX_ORDER = (4, 5, 3, 2, 6, 7, 1)
BAND_ORDER = (4, 5, 3, 2, 6, 7, 1)
RING_ORDER = (4, 3, 5, 2, 6, 1, 7)


def filter_weights(degree):
    half_width = (CUT_HIGH - CUT_LOW) / 2.0
    middle = (CUT_HIGH + CUT_LOW) / 2.0
    sigma = half_width / (LOWER_END - middle)
    tau = 2.0 / sigma
    first = sigma / half_width
    others = []
    for index in range(degree - 1):
        sigma_new = 1.0 / (tau - sigma)
        others.append((2.0 * sigma_new / half_width, sigma * sigma_new))
        sigma = sigma_new
    return (middle, first, others)


def wait_bytes(ref, sem):
    pltpu.make_async_copy(ref, ref, sem).wait()


def dot(a, b, contract):
    return lax.dot_general(
        a,
        b,
        (contract, ((), ())),
        precision=lax.Precision.HIGHEST,
        preferred_element_type=jnp.float32,
    )


def inverse_factor(packed):
    wide = (8, 128)
    lane = lax.broadcasted_iota(jnp.int32, wide, 1)
    sub = lax.broadcasted_iota(jnp.int32, wide, 0)
    rows = []
    for t in range(8):
        part = packed[8 * (t % 4) : 8 * (t % 4) + 8]
        if t >= 4:
            part = pltpu.roll(part, 64, 1)
        unit = jnp.where(lane == sub + 8 * t, 1.0, 0.0)
        rows.append(jnp.where(lane >= 64, part, unit))
    for t in range(8):
        at = 64 + 8 * t
        row = [jnp.broadcast_to(rows[t][j : j + 1, :], wide) for j in range(8)]
        entry = {}
        for j in range(8):
            for l in range(j, 8):
                entry[j, l] = jnp.broadcast_to(rows[t][j : j + 1, at + l : at + l + 1], wide)
        column = {}
        for i in range(t + 1, 8):
            for j in range(8):
                column[i, j] = jnp.broadcast_to(rows[i][:, at + j : at + j + 1], wide)
        scaled = []
        for j in range(8):
            inverse = 1.0 / entry[j, j]
            scaled.append(row[j] * inverse)
            for l in range(j + 1, 8):
                factor = entry[j, l] * inverse
                row[l] = row[l] - factor * row[j]
                for m in range(l, 8):
                    entry[l, m] = entry[l, m] - factor * entry[j, m]
                for i in range(t + 1, 8):
                    column[i, l] = column[i, l] - column[i, j] * factor
        for i in range(t + 1, 8):
            for j in range(8):
                rows[i] = rows[i] - column[i, j] * scaled[j]
        for j in range(1, 8):
            rows[t] = jnp.where(sub == j, row[j], rows[t])
    done = []
    for t in range(8):
        pivots = jnp.sum(jnp.where(lane == sub + (8 * t + 64), rows[t], 0.0), axis=1, keepdims=True)
        done.append(rows[t] * (1.0 / jnp.sqrt(pivots)))
    return jnp.concatenate(done, axis=0)[:, :BANDS]


def kernel(
    start,
    pot,
    out,
    own,
    own_pot,
    turned,
    turned_pot,
    field,
    last,
    pots,
    acc,
    pencil,
    rotated,
    packed,
    half,
    sum_x,
    sum_y,
    sum_z,
    whole,
    local_sem,
    ax_send,
    ax_recv,
    pot_send,
    pot_recv,
    first_send,
    first_recv,
    halo_send,
    halo_recv,
    pen_send,
    pen_recv,
    sum_send,
    sum_recv,
    back_send,
    back_recv,
):
    b = lax.axis_index("band")
    g = lax.axis_index("gx")
    r = lax.axis_index("gy")

    def remote(src, dst, send, recv, device):
        copy = pltpu.make_async_remote_copy(
            src_ref=src, dst_ref=dst, send_sem=send, recv_sem=recv, device_id=device, device_id_type=MESH
        )
        copy.start()
        return copy

    load = pltpu.make_async_copy(start, own, local_sem.at[0])
    load.start()
    load_pot = pltpu.make_async_copy(pot, own_pot, local_sem.at[1])
    load_pot.start()

    plane_peers = [(db, dg) for db in range(NB) for dg in range(NG) if db or dg]
    plane_peers.sort(key=lambda pair: -(2 * min(pair[0] // 2, 4 - pair[0] // 2) + min(pair[1] // 2, 4 - pair[1] // 2)))
    barrier = pltpu.get_barrier_semaphore()
    for db, dg in plane_peers:
        device = {"band": lax.rem(b + db, NB), "gx": lax.rem(g + dg, NG)}
        pl.semaphore_signal(barrier, inc=1, device_id=device, device_id_type=MESH)
    for dy in range(1, NY):
        pl.semaphore_signal(barrier, inc=1, device_id={"gy": lax.rem(r + dy, NY)}, device_id_type=MESH)

    load.wait()
    for i in range(NG):
        for x in range(XW):
            turned[i, :, x, :] = own[i, x]
    load_pot.wait()
    for x in range(XW):
        turned_pot[:, x, :] = own_pot[x]
    pl.semaphore_wait(barrier, len(plane_peers) + NY - 1)

    slot = pl.ds(XW * g, XW)
    for dg in GX_ORDER:
        to = lax.rem(g + dg, NG)
        remote(turned.at[to], field.at[0, pl.ds(REACH, YW), slot, :], ax_send, ax_recv.at[g], {"gx": to})
    copy = pltpu.make_async_copy(turned.at[g], field.at[0, pl.ds(REACH, YW), slot, :], ax_recv.at[g])
    copy.start()
    for dg in GX_ORDER:
        to = lax.rem(g + dg, NG)
        remote(turned_pot, pots.at[:, slot, :], pot_send, pot_recv, {"gx": to})
    copy_pot = pltpu.make_async_copy(turned_pot, pots.at[:, slot, :], local_sem.at[2])
    copy_pot.start()

    up = {"gy": lax.rem(r + 1, NY)}
    down = {"gy": lax.rem(r + NY - 1, NY)}

    def halo(k, cols, send, recv):
        return [
            remote(
                field.at[k, pl.ds(YW, REACH), cols, :],
                field.at[k, pl.ds(0, REACH), cols, :],
                send(0),
                recv(0),
                up,
            ),
            remote(
                field.at[k, pl.ds(REACH, REACH), cols, :],
                field.at[k, pl.ds(YW + REACH, REACH), cols, :],
                send(1),
                recv(1),
                down,
            ),
        ]

    for c in range(CHUNKS):
        for source in range(PIECES[c], PIECES[c + 1]):
            cols = pl.ds(XW * source, XW)
            wait_bytes(field.at[0, pl.ds(REACH, YW), cols, :], ax_recv.at[source])
            halo(0, cols, lambda side: first_send.at[side], lambda side, c=c: first_recv.at[side, c])

    middle, first, others = filter_weights(DEGREE)
    width = NX // CHUNKS
    moves = []
    for k in range(DEGREE):
        scale = first if k == 0 else others[k - 1][0]
        weights = [-0.5 * c * scale for c in COEFFS]

        def local_part(y, carry, k=k, scale=scale, weights=weights):
            plane = field[k, REACH + y]
            total = (3.0 * weights[0] - middle * scale) * plane
            for j in range(1, REACH + 1):
                near = pltpu.roll(plane, j, 0) + pltpu.roll(plane, NX - j, 0)
                near = near + pltpu.roll(plane, j, 1) + pltpu.roll(plane, NZ - j, 1)
                total = total + weights[j] * near
            if k:
                total = total + scale * pots[y] * plane
                total = total - others[k - 1][1] * field[k - 1, REACH + y]
            acc[y] = total
            return carry

        lax.fori_loop(0, YW, local_part, 0)
        if k == 0:
            copy_pot.wait()
            wait_bytes(pots.at[:, pl.ds(0, XW * (NG - 1)), :], pot_recv)
        for y in range(YW):
            total = acc[y]
            if k == 0:
                total = total + scale * pots[y] * field[k, REACH + y]
            for j in range(1, REACH + 1):
                if y - j >= 0:
                    total = total + weights[j] * field[k, REACH + y - j]
                if y + j < YW:
                    total = total + weights[j] * field[k, REACH + y + j]
            acc[y] = total

        later = []
        for c in range(CHUNKS):
            low, high = width * c, width * (c + 1)
            cols = pl.ds(low, width)
            for side in range(2):
                if k:
                    moves[c][side].wait()
                else:
                    got = pl.ds(XW * PIECES[c], XW * (PIECES[c + 1] - PIECES[c]))
                    wait_bytes(field.at[0, pl.ds((YW + REACH) * side, REACH), got, :], first_recv.at[side, c])
            for y in range(YW):
                total = acc[y, low:high]
                for j in range(1, REACH + 1):
                    if y - j < 0:
                        total = total + weights[j] * field[k, REACH + y - j, low:high]
                    if y + j >= YW:
                        total = total + weights[j] * field[k, REACH + y + j, low:high]
                if k < DEGREE - 1:
                    field[k + 1, REACH + y, low:high] = total
                else:
                    last[y, low:high] = total
            if k < DEGREE - 1:
                later.append(
                    halo(
                        k + 1,
                        cols,
                        lambda side, k=k, c=c: halo_send.at[k + 1, side, c],
                        lambda side, k=k, c=c: halo_recv.at[k + 1, side, c],
                    )
                )
        moves = later

    band = NG * b + g
    for db, dg in plane_peers:
        to_b = lax.rem(b + db, NB)
        to_g = lax.rem(g + dg, NG)
        remote(
            last.at[to_b, pl.ds(XW * to_g, XW), :],
            pencil.at[:, band, :],
            pen_send,
            pen_recv,
            {"band": to_b, "gx": to_g},
        )
    copy = pltpu.make_async_copy(last.at[b, pl.ds(XW * g, XW), :], pencil.at[:, band, :], local_sem.at[0])
    copy.start()
    copy.wait()
    wait_bytes(own.at[pl.ds(0, NG - 1)], ax_send)
    wait_bytes(own.at[pl.ds(0, NG - 1)], pot_send)
    for side in range(2):
        wait_bytes(field.at[0, pl.ds((YW + REACH) * side, REACH)], first_send.at[side])
    wait_bytes(pencil.at[:, pl.ds(0, BANDS - 1), :], pen_recv)

    cells = jnp.concatenate([pencil[x] for x in range(XW)], axis=1)
    twice = jnp.concatenate([cells, cells], axis=0)
    products = dot(cells, twice, ((1,), (1,)))
    lane = lax.broadcasted_iota(jnp.int32, (32, 128), 1)
    joined = jnp.where(lane < 64, products[32:], products[:32])
    packed[0] = joined[:16]
    packed[1] = joined[16:]

    core = lax.rem(b, 2)
    zhi, zlo, chip_x = b // 2, lax.rem(g, 2), g // 2
    place = 2 * zhi + zlo
    partner = {"band": b + 1 - 2 * core}

    def along(index, first_axis):
        return {
            "band": (1 - first_axis) * b + first_axis * (2 * (index // 2) + core),
            "gx": (1 - first_axis) * g + first_axis * (2 * chip_x + lax.rem(index, 2)),
            "gy": (1 - first_axis) * index + first_axis * r,
        }

    def spread(table, value, index, stage, offsets, device_of):
        count = len(offsets)
        table[index] = value
        for d in offsets:
            remote(
                table.at[index],
                table.at[index],
                sum_send.at[stage],
                sum_recv.at[stage],
                device_of(lax.rem(index + d, count + 1)),
            )
        wait_bytes(table.at[pl.ds(0, count)], sum_recv.at[stage])
        parts = [table[i] for i in range(count + 1)]
        while len(parts) > 1:
            parts = [parts[i] + parts[i + 1] for i in range(0, len(parts), 2)]
        return parts[0]

    remote(packed.at[1 - core], half, sum_send.at[0], sum_recv.at[0], partner)
    wait_bytes(half, sum_recv.at[0])
    value = packed[core] + half[...]
    value = spread(sum_x, value, chip_x, 1, (2, 1, 3), lambda i: {"gx": 2 * i + zlo})
    mine = (1 - core) * r + core * place
    value = spread(sum_y, value, mine, 2, RING_ORDER, lambda i: along(i, core))
    mine = (1 - core) * place + core * r
    value = spread(sum_z, value, mine, 3, RING_ORDER, lambda i: along(i, 1 - core))
    whole[core] = value * (1.0 / CELLS)
    remote(whole.at[core], whole.at[core], sum_send.at[4], sum_recv.at[4], partner)
    wait_bytes(half, sum_recv.at[4])

    inverse = inverse_factor(whole[...].reshape(32, 128))
    for x in range(XW):
        turn = dot(inverse, pencil[x], ((1,), (0,)))
        for i in range(NB):
            rotated[i, :, x, :] = turn[8 * i : 8 * i + 8]

    for db in BAND_ORDER:
        to = lax.rem(b + db, NB)
        remote(rotated.at[to], out.at[:, :, b, :], back_send, back_recv, {"band": to})
    copy = pltpu.make_async_copy(rotated.at[b], out.at[:, :, b, :], local_sem.at[1])
    copy.start()
    wait_bytes(pencil.at[:, pl.ds(0, BANDS - 1), :], pen_send)
    for stage, table in ((1, sum_x.at[pl.ds(0, 3)]), (2, sum_y.at[pl.ds(0, 7)]), (3, sum_z.at[pl.ds(0, 7)])):
        wait_bytes(table, sum_send.at[stage])
    wait_bytes(half, sum_send.at[0])
    wait_bytes(half, sum_send.at[4])
    copy.wait()
    wait_bytes(own.at[pl.ds(0, NB - 1)], back_recv)
    wait_bytes(own.at[pl.ds(0, NB - 1)], back_send)


def on_device(start_bands, potential):
    f32 = jnp.float32
    dma = pltpu.SemaphoreType.DMA
    return pl.pallas_call(
        kernel,
        out_shape=jax.ShapeDtypeStruct((8, XW, YW, NZ), f32),
        in_specs=[pl.BlockSpec(memory_space=pl.ANY)] * 2,
        out_specs=pl.BlockSpec(memory_space=pl.ANY),
        scratch_shapes=[
            pltpu.VMEM((8, XW, YW, NZ), f32),
            pltpu.VMEM((XW, YW, NZ), f32),
            pltpu.VMEM((8, YW, XW, NZ), f32),
            pltpu.VMEM((YW, XW, NZ), f32),
            pltpu.VMEM((DEGREE, YW + 2 * REACH, NX, NZ), f32),
            pltpu.VMEM((YW, NX, NZ), f32),
            pltpu.VMEM((YW, NX, NZ), f32),
            pltpu.VMEM((YW, NX, NZ), f32),
            pltpu.VMEM((XW, BANDS, NZ), f32),
            pltpu.VMEM((NB, 8, XW, NZ), f32),
            pltpu.VMEM((2, 16, 128), f32),
            pltpu.VMEM((16, 128), f32),
            pltpu.VMEM((4, 16, 128), f32),
            pltpu.VMEM((8, 16, 128), f32),
            pltpu.VMEM((8, 16, 128), f32),
            pltpu.VMEM((2, 16, 128), f32),
            dma((3,)),
            dma,
            dma((NG,)),
            dma,
            dma,
            dma((2,)),
            dma((2, CHUNKS)),
            dma((DEGREE, 2, CHUNKS)),
            dma((DEGREE, 2, CHUNKS)),
            dma,
            dma,
            dma((5,)),
            dma((5,)),
            dma,
            dma,
        ],
        compiler_params=pltpu.CompilerParams(collective_id=0, has_side_effects=True),
    )(start_bands, potential)


def solution(mesh):
    in_specs = (P("band", "gx", "gy", None), P("gx", "gy", None))
    out_specs = P("band", "gx", "gy", None)
    return jax.shard_map(on_device, mesh=mesh, in_specs=in_specs, out_specs=out_specs, check_vma=False)
```

```python
import jax
import jax.numpy as jnp
from jax import lax
from jax.experimental import pallas as pl
from jax.experimental.pallas import tpu as pltpu
from jax.sharding import PartitionSpec as P

DEGREE = 4
COEFFS = (
    -5369.0 / 1800.0,
    12.0 / 7.0,
    -15.0 / 56.0,
    10.0 / 189.0,
    -1.0 / 112.0,
    2.0 / 1925.0,
    -1.0 / 16632.0,
)
LOWER_END = -0.5
CUT_LOW = 3.0
CUT_HIGH = 12.7
REACH = 6
MESH = pl.DeviceIdType.MESH
NB, NG, NY = 8, 8, 8
XW, YW, NX, NZ = 6, 8, 48, 128
BANDS = 64
CELLS = 48 * 64 * 128
CHUNKS = 3
PIECES = {2: (0, 4, 8), 3: (0, 3, 6, 8)}[CHUNKS]
GX_ORDER = (4, 5, 3, 2, 6, 7, 1)
BAND_ORDER = (4, 5, 3, 2, 6, 7, 1)
RING_ORDER = (4, 3, 5, 2, 6, 1, 7)


def filter_weights(degree):
    half_width = (CUT_HIGH - CUT_LOW) / 2.0
    middle = (CUT_HIGH + CUT_LOW) / 2.0
    sigma = half_width / (LOWER_END - middle)
    tau = 2.0 / sigma
    first = sigma / half_width
    others = []
    for index in range(degree - 1):
        sigma_new = 1.0 / (tau - sigma)
        others.append((2.0 * sigma_new / half_width, sigma * sigma_new))
        sigma = sigma_new
    return (middle, first, others)


def wait_bytes(ref, sem):
    pltpu.make_async_copy(ref, ref, sem).wait()


def dot(a, b, contract):
    return lax.dot_general(
        a,
        b,
        (contract, ((), ())),
        precision=lax.Precision.HIGHEST,
        preferred_element_type=jnp.float32,
    )


def inverse_factor(packed):
    wide = (8, 128)
    lane = lax.broadcasted_iota(jnp.int32, wide, 1)
    sub = lax.broadcasted_iota(jnp.int32, wide, 0)
    rows = []
    for t in range(8):
        part = packed[8 * (t % 4) : 8 * (t % 4) + 8]
        if t >= 4:
            part = pltpu.roll(part, 64, 1)
        unit = jnp.where(lane == sub + 8 * t, 1.0, 0.0)
        rows.append(jnp.where(lane >= 64, part, unit))
    for t in range(8):
        at = 64 + 8 * t
        row = [jnp.broadcast_to(rows[t][j : j + 1, :], wide) for j in range(8)]
        entry = {}
        for j in range(8):
            for l in range(j, 8):
                entry[j, l] = jnp.broadcast_to(rows[t][j : j + 1, at + l : at + l + 1], wide)
        column = {}
        for i in range(t + 1, 8):
            for j in range(8):
                column[i, j] = jnp.broadcast_to(rows[i][:, at + j : at + j + 1], wide)
        scaled = []
        for j in range(8):
            inverse = 1.0 / entry[j, j]
            scaled.append(row[j] * inverse)
            for l in range(j + 1, 8):
                factor = entry[j, l] * inverse
                row[l] = row[l] - factor * row[j]
                for m in range(l, 8):
                    entry[l, m] = entry[l, m] - factor * entry[j, m]
                for i in range(t + 1, 8):
                    column[i, l] = column[i, l] - column[i, j] * factor
        for i in range(t + 1, 8):
            for j in range(8):
                rows[i] = rows[i] - column[i, j] * scaled[j]
        for j in range(1, 8):
            rows[t] = jnp.where(sub == j, row[j], rows[t])
    done = []
    for t in range(8):
        pivots = jnp.sum(jnp.where(lane == sub + (8 * t + 64), rows[t], 0.0), axis=1, keepdims=True)
        done.append(rows[t] * (1.0 / jnp.sqrt(pivots)))
    return jnp.concatenate(done, axis=0)[:, :BANDS]


def kernel(
    start,
    pot,
    out,
    own,
    own_pot,
    turned,
    turned_pot,
    field,
    last,
    pots,
    acc,
    pencil,
    rotated,
    packed,
    sum_x,
    sum_y,
    whole,
    ready,
    local_sem,
    ax_send,
    ax_recv,
    pot_send,
    pot_recv,
    first_send,
    first_recv,
    halo_send,
    halo_recv,
    pen_send,
    pen_recv,
    sum_send,
    sum_recv,
    back_send,
    back_recv,
):
    b = lax.axis_index("band")
    g = lax.axis_index("gx")
    r = lax.axis_index("gy")

    def remote(src, dst, send, recv, device):
        copy = pltpu.make_async_remote_copy(
            src_ref=src, dst_ref=dst, send_sem=send, recv_sem=recv, device_id=device, device_id_type=MESH
        )
        copy.start()
        return copy

    load = pltpu.make_async_copy(start, own, local_sem.at[0])
    load.start()
    load_pot = pltpu.make_async_copy(pot, own_pot, local_sem.at[1])
    load_pot.start()

    plane_peers = [(db, dg) for db in range(NB) for dg in range(NG) if db or dg]
    plane_peers.sort(key=lambda pair: -(2 * min(pair[0] // 2, 4 - pair[0] // 2) + min(pair[1] // 2, 4 - pair[1] // 2)))
    barrier = pltpu.get_barrier_semaphore()
    core = lax.rem(b, 2)
    zhi, zlo, chip_x = b // 2, lax.rem(g, 2), g // 2
    partner = {"band": b + 1 - 2 * core}
    beside = [{"band": lax.rem(b + db, NB)} for db in (2, NB - 2)]
    greeted = beside + [partner]
    greeted += [{"gx": lax.rem(g + dg, NG)} for dg in GX_ORDER]
    greeted += [{"gy": lax.rem(r + dy, NY)} for dy in (1, NY - 1)]
    for device in greeted:
        pl.semaphore_signal(barrier, inc=1, device_id=device, device_id_type=MESH)

    load.wait()
    for i in range(NG):
        for x in range(XW):
            turned[i, :, x, :] = own[i, x]
    load_pot.wait()
    for x in range(XW):
        turned_pot[:, x, :] = own_pot[x]
    pl.semaphore_wait(barrier, len(greeted))

    slot = pl.ds(XW * g, XW)
    for dg in GX_ORDER:
        to = lax.rem(g + dg, NG)
        remote(turned.at[to], field.at[0, pl.ds(REACH, YW), slot, :], ax_send, ax_recv.at[g], {"gx": to})
    copy = pltpu.make_async_copy(turned.at[g], field.at[0, pl.ds(REACH, YW), slot, :], ax_recv.at[g])
    copy.start()

    up = {"gy": lax.rem(r + 1, NY)}
    down = {"gy": lax.rem(r + NY - 1, NY)}

    def halo(k, cols, send, recv):
        return [
            remote(
                field.at[k, pl.ds(YW, REACH), cols, :],
                field.at[k, pl.ds(0, REACH), cols, :],
                send(0),
                recv(0),
                up,
            ),
            remote(
                field.at[k, pl.ds(REACH, REACH), cols, :],
                field.at[k, pl.ds(YW + REACH, REACH), cols, :],
                send(1),
                recv(1),
                down,
            ),
        ]

    for c in range(CHUNKS):
        for source in range(PIECES[c], PIECES[c + 1]):
            cols = pl.ds(XW * source, XW)
            wait_bytes(field.at[0, pl.ds(REACH, YW), cols, :], ax_recv.at[source])
            halo(0, cols, lambda side: first_send.at[side], lambda side, c=c: first_recv.at[side, c])

    for dg in GX_ORDER:
        to = lax.rem(g + dg, NG)
        remote(turned_pot, pots.at[:, slot, :], pot_send, pot_recv, {"gx": to})
    copy_pot = pltpu.make_async_copy(turned_pot, pots.at[:, slot, :], local_sem.at[2])
    copy_pot.start()

    def tell(devices, round_):
        for device in devices:
            pl.semaphore_signal(ready.at[round_], inc=1, device_id=device, device_id_type=MESH)

    tell(beside, 0)

    middle, first, others = filter_weights(DEGREE)
    width = NX // CHUNKS
    factors = []
    for k in range(DEGREE):
        scale = first if k == 0 else others[k - 1][0]
        factors.append((scale, [-0.5 * c * scale for c in COEFFS]))

    def side_part(k, low, high):
        scale, weights = factors[k]
        for y in range(YW):
            plane = field[k, REACH + y, low:high]
            total = (3.0 * weights[0] - middle * scale) * plane
            if k:
                total = total + scale * pots[y, low:high] * plane
                total = total - others[k - 1][1] * field[k - 1, REACH + y, low:high]
            for j in range(1, REACH + 1):
                near = pltpu.roll(plane, j, 1) + pltpu.roll(plane, NZ - j, 1)
                if y - j >= 0:
                    near = near + field[k, REACH + y - j, low:high]
                if y + j < YW:
                    near = near + field[k, REACH + y + j, low:high]
                total = total + weights[j] * near
            acc[y, low:high] = total

    def x_part(k):
        weights = factors[k][1]

        def planes(i, carry):
            for y in (2 * i, 2 * i + 1):
                plane = field[k, REACH + y]
                total = acc[y]
                for j in range(1, REACH + 1):
                    total = total + weights[j] * (pltpu.roll(plane, j, 0) + pltpu.roll(plane, NX - j, 0))
                acc[y] = total
            return carry

        lax.fori_loop(0, YW // 2, planes, 0)

    moves = []
    for c in range(CHUNKS):
        side_part(0, width * c, width * (c + 1))
    for k in range(DEGREE):
        scale, weights = factors[k]
        x_part(k)
        if k == 0:
            copy_pot.wait()
            wait_bytes(pots.at[:, pl.ds(0, XW * (NG - 1)), :], pot_recv)
            for y in range(YW):
                acc[y] = acc[y] + scale * pots[y] * field[0, REACH + y]
        later = []
        for c in range(CHUNKS):
            low, high = width * c, width * (c + 1)
            cols = pl.ds(low, width)
            for side in range(2):
                if k:
                    moves[c][side].wait()
                else:
                    got = pl.ds(XW * PIECES[c], XW * (PIECES[c + 1] - PIECES[c]))
                    wait_bytes(field.at[0, pl.ds((YW + REACH) * side, REACH), got, :], first_recv.at[side, c])
            for y in range(YW):
                total = acc[y, low:high]
                for j in range(1, REACH + 1):
                    if y - j < 0:
                        total = total + weights[j] * field[k, REACH + y - j, low:high]
                    if y + j >= YW:
                        total = total + weights[j] * field[k, REACH + y + j, low:high]
                if k < DEGREE - 1:
                    field[k + 1, REACH + y, low:high] = total
                else:
                    last[y, low:high] = total
            if k < DEGREE - 1:
                later.append(
                    halo(
                        k + 1,
                        cols,
                        lambda side, k=k, c=c: halo_send.at[k + 1, side, c],
                        lambda side, k=k, c=c: halo_recv.at[k + 1, side, c],
                    )
                )
                side_part(k + 1, low, high)
        moves = later
        if k == 0:
            pl.semaphore_wait(ready.at[0], len(beside))
            tell([partner], 1)
        if k == 1:
            pl.semaphore_wait(ready.at[1], 1)
            tell([{"gx": lax.rem(g + dg, NG)} for dg in GX_ORDER], 2)

    pl.semaphore_wait(ready.at[2], NG - 1)
    band = NG * b + g
    for db, dg in plane_peers:
        to_b = lax.rem(b + db, NB)
        to_g = lax.rem(g + dg, NG)
        remote(
            last.at[to_b, pl.ds(XW * to_g, XW), :],
            pencil.at[:, band, :],
            pen_send,
            pen_recv,
            {"band": to_b, "gx": to_g},
        )
    copy = pltpu.make_async_copy(last.at[b, pl.ds(XW * g, XW), :], pencil.at[:, band, :], local_sem.at[0])
    copy.start()
    copy.wait()
    wait_bytes(own.at[pl.ds(0, NG - 1)], ax_send)
    wait_bytes(own.at[pl.ds(0, NG - 1)], pot_send)
    for side in range(2):
        wait_bytes(field.at[0, pl.ds((YW + REACH) * side, REACH)], first_send.at[side])
    wait_bytes(pencil.at[:, pl.ds(0, BANDS - 1), :], pen_recv)

    cells = jnp.concatenate([pencil[x] for x in range(XW)], axis=1)
    twice = jnp.concatenate([cells, cells], axis=0)
    products = dot(cells, twice, ((1,), (1,)))
    lane = lax.broadcasted_iota(jnp.int32, (32, 128), 1)
    joined = jnp.where(lane < 64, products[32:], products[:32])
    packed[0] = joined[:16]
    packed[1] = joined[16:]

    piece = 2 * chip_x + core
    place = 2 * zhi + zlo

    def added(table, start_at=0):
        parts = [table[start_at + i] for i in range(8)]
        while len(parts) > 1:
            parts = [parts[i] + parts[i + 1] for i in range(0, len(parts), 2)]
        return parts[0]

    def along(index, axis, to_core):
        return {
            "band": 2 * ((1 - axis) * zhi + axis * (index // 2)) + to_core,
            "gx": (1 - axis) * g + axis * (2 * chip_x + lax.rem(index, 2)),
            "gy": (1 - axis) * index + axis * r,
        }

    for d in GX_ORDER:
        other = lax.rem(piece + d, 8)
        to_core = lax.rem(other, 2)
        remote(
            packed.at[to_core],
            sum_x.at[piece],
            sum_send.at[0],
            sum_recv.at[0],
            {"band": 2 * zhi + to_core, "gx": 2 * (other // 2) + zlo},
        )
    sum_x[piece] = packed[core]
    wait_bytes(sum_x.at[pl.ds(0, 7)], sum_recv.at[0])

    mine = (1 - core) * r + core * place
    sum_y[mine] = added(sum_x)
    for d in RING_ORDER:
        to = along(lax.rem(mine + d, 8), core, core)
        remote(sum_y.at[mine], sum_y.at[mine], sum_send.at[1], sum_recv.at[1], to)
    wait_bytes(sum_y.at[pl.ds(0, 7)], sum_recv.at[1])

    mine = (1 - core) * place + core * r
    row = 8 * core + mine
    whole[row] = added(sum_y)
    for d in RING_ORDER + (0,):
        for to_core in (1 - core, core)[: 2 if d else 1]:
            to = along(lax.rem(mine + d, 8), 1 - core, to_core)
            remote(whole.at[row], whole.at[row], sum_send.at[2], sum_recv.at[2], to)
    wait_bytes(whole.at[pl.ds(0, 15)], sum_recv.at[2])
    margin = jnp.concatenate([added(whole, 0), added(whole, 8)], axis=0) * (1.0 / CELLS)

    inverse = inverse_factor(margin)
    for x in range(XW):
        turn = dot(inverse, pencil[x], ((1,), (0,)))
        for i in range(NB):
            rotated[i, :, x, :] = turn[8 * i : 8 * i + 8]

    for db in BAND_ORDER:
        to = lax.rem(b + db, NB)
        remote(rotated.at[to], out.at[:, :, b, :], back_send, back_recv, {"band": to})
    copy = pltpu.make_async_copy(rotated.at[b], out.at[:, :, b, :], local_sem.at[1])
    copy.start()
    wait_bytes(pencil.at[:, pl.ds(0, BANDS - 1), :], pen_send)
    for stage, table in enumerate((sum_x.at[pl.ds(0, 7)], sum_y.at[pl.ds(0, 7)], whole.at[pl.ds(0, 15)])):
        wait_bytes(table, sum_send.at[stage])
    copy.wait()
    wait_bytes(own.at[pl.ds(0, NB - 1)], back_recv)
    wait_bytes(own.at[pl.ds(0, NB - 1)], back_send)


def on_device(start_bands, potential):
    f32 = jnp.float32
    dma = pltpu.SemaphoreType.DMA
    return pl.pallas_call(
        kernel,
        out_shape=jax.ShapeDtypeStruct((8, XW, YW, NZ), f32),
        in_specs=[pl.BlockSpec(memory_space=pl.ANY)] * 2,
        out_specs=pl.BlockSpec(memory_space=pl.ANY),
        scratch_shapes=[
            pltpu.VMEM((8, XW, YW, NZ), f32),
            pltpu.VMEM((XW, YW, NZ), f32),
            pltpu.VMEM((8, YW, XW, NZ), f32),
            pltpu.VMEM((YW, XW, NZ), f32),
            pltpu.VMEM((DEGREE, YW + 2 * REACH, NX, NZ), f32),
            pltpu.VMEM((YW, NX, NZ), f32),
            pltpu.VMEM((YW, NX, NZ), f32),
            pltpu.VMEM((YW, NX, NZ), f32),
            pltpu.VMEM((XW, BANDS, NZ), f32),
            pltpu.VMEM((NB, 8, XW, NZ), f32),
            pltpu.VMEM((2, 16, 128), f32),
            pltpu.VMEM((8, 16, 128), f32),
            pltpu.VMEM((8, 16, 128), f32),
            pltpu.VMEM((16, 16, 128), f32),
            pltpu.SemaphoreType.REGULAR((3,)),
            dma((3,)),
            dma,
            dma((NG,)),
            dma,
            dma,
            dma((2,)),
            dma((2, CHUNKS)),
            dma((DEGREE, 2, CHUNKS)),
            dma((DEGREE, 2, CHUNKS)),
            dma,
            dma,
            dma((3,)),
            dma((3,)),
            dma,
            dma,
        ],
        compiler_params=pltpu.CompilerParams(
            collective_id=0, has_side_effects=True, vmem_limit_bytes=24 * 1024 * 1024
        ),
    )(*[pltpu.with_memory_space_constraint(value, pltpu.HBM) for value in (start_bands, potential)])


def solution(mesh):
    in_specs = (P("band", "gx", "gy", None), P("gx", "gy", None))
    out_specs = P("band", "gx", "gy", None)
    return jax.shard_map(on_device, mesh=mesh, in_specs=in_specs, out_specs=out_specs, check_vma=False)
```

```python
import jax
import jax.numpy as jnp
from jax import lax
from jax.experimental import pallas as pl
from jax.experimental.pallas import tpu as pltpu
from jax.sharding import PartitionSpec as P

DEGREE = 4
COEFFS = (
    -5369.0 / 1800.0,
    12.0 / 7.0,
    -15.0 / 56.0,
    10.0 / 189.0,
    -1.0 / 112.0,
    2.0 / 1925.0,
    -1.0 / 16632.0,
)
LOWER_END = -0.5
CUT_LOW = 3.0
CUT_HIGH = 12.7
REACH = 6
MESH = pl.DeviceIdType.MESH
NB, NG, NY = 8, 8, 8
XW, YW, NX, NZ = 6, 8, 48, 128
BANDS = 64
CELLS = 48 * 64 * 128
CHUNKS = 3
PIECES = {2: (0, 4, 8), 3: (0, 3, 6, 8)}[CHUNKS]
GX_ORDER = (4, 5, 3, 2, 6, 7, 1)
BAND_ORDER = (4, 5, 3, 2, 6, 7, 1)
RING_ORDER = (4, 3, 5, 2, 6, 1, 7)


def filter_weights(degree):
    half_width = (CUT_HIGH - CUT_LOW) / 2.0
    middle = (CUT_HIGH + CUT_LOW) / 2.0
    sigma = half_width / (LOWER_END - middle)
    tau = 2.0 / sigma
    first = sigma / half_width
    others = []
    for index in range(degree - 1):
        sigma_new = 1.0 / (tau - sigma)
        others.append((2.0 * sigma_new / half_width, sigma * sigma_new))
        sigma = sigma_new
    return (middle, first, others)


def wait_bytes(ref, sem):
    pltpu.make_async_copy(ref, ref, sem).wait()


def dot(a, b, contract):
    return lax.dot_general(
        a,
        b,
        (contract, ((), ())),
        precision=lax.Precision.HIGHEST,
        preferred_element_type=jnp.float32,
    )


def inverse_factor(packed):
    wide = (8, 128)
    lane = lax.broadcasted_iota(jnp.int32, wide, 1)
    sub = lax.broadcasted_iota(jnp.int32, wide, 0)
    rows = []
    for t in range(8):
        part = packed[8 * (t % 4) : 8 * (t % 4) + 8]
        if t >= 4:
            part = pltpu.roll(part, 64, 1)
        unit = jnp.where(lane == sub + 8 * t, 1.0, 0.0)
        rows.append(jnp.where(lane >= 64, part, unit))
    for t in range(8):
        at = 64 + 8 * t
        row = [jnp.broadcast_to(rows[t][j : j + 1, :], wide) for j in range(8)]
        entry = {}
        for j in range(8):
            for l in range(j, 8):
                entry[j, l] = jnp.broadcast_to(rows[t][j : j + 1, at + l : at + l + 1], wide)
        column = {}
        for i in range(t + 1, 8):
            for j in range(8):
                column[i, j] = jnp.broadcast_to(rows[i][:, at + j : at + j + 1], wide)
        scaled = []
        for j in range(8):
            inverse = 1.0 / entry[j, j]
            scaled.append(row[j] * inverse)
            for l in range(j + 1, 8):
                factor = entry[j, l] * inverse
                row[l] = row[l] - factor * row[j]
                for m in range(l, 8):
                    entry[l, m] = entry[l, m] - factor * entry[j, m]
                for i in range(t + 1, 8):
                    column[i, l] = column[i, l] - column[i, j] * factor
        for i in range(t + 1, 8):
            for j in range(8):
                rows[i] = rows[i] - column[i, j] * scaled[j]
        for j in range(1, 8):
            rows[t] = jnp.where(sub == j, row[j], rows[t])
    done = []
    for t in range(8):
        pivots = jnp.sum(jnp.where(lane == sub + (8 * t + 64), rows[t], 0.0), axis=1, keepdims=True)
        done.append(rows[t] * (1.0 / jnp.sqrt(pivots)))
    return jnp.concatenate(done, axis=0)[:, :BANDS]


def kernel(
    start,
    pot,
    out,
    own,
    own_pot,
    turned,
    turned_pot,
    field,
    last,
    pots,
    acc,
    pencil,
    rotated,
    packed,
    sum_x,
    sum_y,
    whole,
    ready,
    local_sem,
    ax_send,
    ax_recv,
    pot_send,
    pot_recv,
    first_send,
    first_recv,
    halo_send,
    halo_recv,
    pen_send,
    pen_recv,
    sum_send,
    sum_recv,
    back_send,
    back_recv,
):
    b = lax.axis_index("band")
    g = lax.axis_index("gx")
    r = lax.axis_index("gy")

    def remote(src, dst, send, recv, device):
        copy = pltpu.make_async_remote_copy(
            src_ref=src, dst_ref=dst, send_sem=send, recv_sem=recv, device_id=device, device_id_type=MESH
        )
        copy.start()
        return copy

    load = pltpu.make_async_copy(start, own, local_sem.at[0])
    load.start()
    load_pot = pltpu.make_async_copy(pot, own_pot, local_sem.at[1])
    load_pot.start()

    barrier = pltpu.get_barrier_semaphore()
    core = lax.rem(b, 2)
    zhi, zlo, chip_x = b // 2, lax.rem(g, 2), g // 2
    partner = {"band": b + 1 - 2 * core}
    beside = [{"band": lax.rem(b + db, NB)} for db in (2, NB - 2)]
    greeted = beside + [partner]
    greeted += [{"gx": lax.rem(g + dg, NG)} for dg in GX_ORDER]
    greeted += [{"gy": lax.rem(r + dy, NY)} for dy in (1, NY - 1)]
    for device in greeted:
        pl.semaphore_signal(barrier, inc=1, device_id=device, device_id_type=MESH)

    load.wait()
    for i in range(NG):
        for x in range(XW):
            turned[i, :, x, :] = own[i, x]
    load_pot.wait()
    for x in range(XW):
        turned_pot[:, x, :] = own_pot[x]
    pl.semaphore_wait(barrier, len(greeted))

    slot = pl.ds(XW * g, XW)
    for dg in GX_ORDER:
        to = lax.rem(g + dg, NG)
        remote(turned.at[to], field.at[0, pl.ds(REACH, YW), slot, :], ax_send, ax_recv.at[g], {"gx": to})
    copy = pltpu.make_async_copy(turned.at[g], field.at[0, pl.ds(REACH, YW), slot, :], ax_recv.at[g])
    copy.start()

    up = {"gy": lax.rem(r + 1, NY)}
    down = {"gy": lax.rem(r + NY - 1, NY)}

    def halo(k, cols, send, recv):
        return [
            remote(
                field.at[k, pl.ds(YW, REACH), cols, :],
                field.at[k, pl.ds(0, REACH), cols, :],
                send(0),
                recv(0),
                up,
            ),
            remote(
                field.at[k, pl.ds(REACH, REACH), cols, :],
                field.at[k, pl.ds(YW + REACH, REACH), cols, :],
                send(1),
                recv(1),
                down,
            ),
        ]

    for c in range(CHUNKS):
        for source in range(PIECES[c], PIECES[c + 1]):
            cols = pl.ds(XW * source, XW)
            wait_bytes(field.at[0, pl.ds(REACH, YW), cols, :], ax_recv.at[source])
            halo(0, cols, lambda side: first_send.at[side], lambda side, c=c: first_recv.at[side, c])

    for dg in GX_ORDER:
        to = lax.rem(g + dg, NG)
        remote(turned_pot, pots.at[:, slot, :], pot_send, pot_recv, {"gx": to})
    copy_pot = pltpu.make_async_copy(turned_pot, pots.at[:, slot, :], local_sem.at[2])
    copy_pot.start()

    def tell(devices, round_):
        for device in devices:
            pl.semaphore_signal(ready.at[round_], inc=1, device_id=device, device_id_type=MESH)

    tell(beside, 0)

    middle, first, others = filter_weights(DEGREE)
    width = NX // CHUNKS
    factors = []
    for k in range(DEGREE):
        scale = first if k == 0 else others[k - 1][0]
        factors.append((scale, [-0.5 * c * scale for c in COEFFS]))

    def side_part(k, low, high):
        scale, weights = factors[k]
        for y in range(YW):
            plane = field[k, REACH + y, low:high]
            total = (3.0 * weights[0] - middle * scale) * plane
            if k:
                total = total + scale * pots[y, low:high] * plane
                total = total - others[k - 1][1] * field[k - 1, REACH + y, low:high]
            for j in range(1, REACH + 1):
                near = pltpu.roll(plane, j, 1) + pltpu.roll(plane, NZ - j, 1)
                if y - j >= 0:
                    near = near + field[k, REACH + y - j, low:high]
                if y + j < YW:
                    near = near + field[k, REACH + y + j, low:high]
                total = total + weights[j] * near
            acc[y, low:high] = total

    def x_part(k):
        weights = factors[k][1]

        def planes(i, carry):
            for y in (2 * i, 2 * i + 1):
                plane = field[k, REACH + y]
                total = acc[y]
                for j in range(1, REACH + 1):
                    total = total + weights[j] * (pltpu.roll(plane, j, 0) + pltpu.roll(plane, NX - j, 0))
                acc[y] = total
            return carry

        lax.fori_loop(0, YW // 2, planes, 0)

    band = NG * b + g

    def pass_on(to_g):
        for db in BAND_ORDER + (0,):
            to_b = lax.rem(b + db, NB)
            src = last.at[to_b, pl.ds(XW * to_g, XW), :]
            dst = pencil.at[:, band, :]

            def send(src=src, dst=dst, to_b=to_b):
                remote(src, dst, pen_send, pen_recv, {"band": to_b, "gx": to_g})

            if db:
                send()
            else:
                pl.when(g != to_g)(send)

                @pl.when(g == to_g)
                def _(src=src, dst=dst):
                    pltpu.make_async_copy(src, dst, local_sem.at[0]).start()

    moves = []
    for c in range(CHUNKS):
        side_part(0, width * c, width * (c + 1))
    for k in range(DEGREE):
        scale, weights = factors[k]
        x_part(k)
        if k == 0:
            copy_pot.wait()
            wait_bytes(pots.at[:, pl.ds(0, XW * (NG - 1)), :], pot_recv)
            for y in range(YW):
                acc[y] = acc[y] + scale * pots[y] * field[0, REACH + y]
        later = []
        for c in range(CHUNKS):
            low, high = width * c, width * (c + 1)
            cols = pl.ds(low, width)
            for side in range(2):
                if k:
                    moves[c][side].wait()
                else:
                    got = pl.ds(XW * PIECES[c], XW * (PIECES[c + 1] - PIECES[c]))
                    wait_bytes(field.at[0, pl.ds((YW + REACH) * side, REACH), got, :], first_recv.at[side, c])
            for y in range(YW):
                total = acc[y, low:high]
                for j in range(1, REACH + 1):
                    if y - j < 0:
                        total = total + weights[j] * field[k, REACH + y - j, low:high]
                    if y + j >= YW:
                        total = total + weights[j] * field[k, REACH + y + j, low:high]
                if k < DEGREE - 1:
                    field[k + 1, REACH + y, low:high] = total
                else:
                    last[y, low:high] = total
            if k < DEGREE - 1:
                later.append(
                    halo(
                        k + 1,
                        cols,
                        lambda side, k=k, c=c: halo_send.at[k + 1, side, c],
                        lambda side, k=k, c=c: halo_recv.at[k + 1, side, c],
                    )
                )
                side_part(k + 1, low, high)
            else:
                if c == 0:
                    pl.semaphore_wait(ready.at[2], NG - 1)
                for to_g in range(low // XW, high // XW):
                    pass_on(to_g)
        moves = later
        if k == 0:
            pl.semaphore_wait(ready.at[0], len(beside))
            tell([partner], 1)
        if k == 1:
            pl.semaphore_wait(ready.at[1], 1)
            tell([{"gx": lax.rem(g + dg, NG)} for dg in GX_ORDER], 2)

    wait_bytes(pencil.at[:, 0, :], local_sem.at[0])
    wait_bytes(own.at[pl.ds(0, NG - 1)], ax_send)
    wait_bytes(own.at[pl.ds(0, NG - 1)], pot_send)
    for side in range(2):
        wait_bytes(field.at[0, pl.ds((YW + REACH) * side, REACH)], first_send.at[side])
    wait_bytes(pencil.at[:, pl.ds(0, BANDS - 1), :], pen_recv)

    cells = jnp.concatenate([pencil[x] for x in range(XW)], axis=1)
    twice = jnp.concatenate([cells, cells], axis=0)
    products = dot(cells, twice, ((1,), (1,)))
    lane = lax.broadcasted_iota(jnp.int32, (32, 128), 1)
    joined = jnp.where(lane < 64, products[32:], products[:32])
    packed[0] = joined[:16]
    packed[1] = joined[16:]

    piece = 2 * chip_x + core
    place = 2 * zhi + zlo

    def added(table, start_at=0):
        parts = [table[start_at + i] for i in range(8)]
        while len(parts) > 1:
            parts = [parts[i] + parts[i + 1] for i in range(0, len(parts), 2)]
        return parts[0]

    def along(index, axis, to_core):
        return {
            "band": 2 * ((1 - axis) * zhi + axis * (index // 2)) + to_core,
            "gx": (1 - axis) * g + axis * (2 * chip_x + lax.rem(index, 2)),
            "gy": (1 - axis) * index + axis * r,
        }

    for d in GX_ORDER:
        other = lax.rem(piece + d, 8)
        to_core = lax.rem(other, 2)
        remote(
            packed.at[to_core],
            sum_x.at[piece],
            sum_send.at[0],
            sum_recv.at[0],
            {"band": 2 * zhi + to_core, "gx": 2 * (other // 2) + zlo},
        )
    sum_x[piece] = packed[core]
    wait_bytes(sum_x.at[pl.ds(0, 7)], sum_recv.at[0])

    mine = (1 - core) * r + core * place
    sum_y[mine] = added(sum_x)
    for d in RING_ORDER:
        to = along(lax.rem(mine + d, 8), core, core)
        remote(sum_y.at[mine], sum_y.at[mine], sum_send.at[1], sum_recv.at[1], to)
    wait_bytes(sum_y.at[pl.ds(0, 7)], sum_recv.at[1])

    mine = (1 - core) * place + core * r
    row = 8 * core + mine
    whole[row] = added(sum_y)
    for d in RING_ORDER + (0,):
        for to_core in (1 - core, core)[: 2 if d else 1]:
            to = along(lax.rem(mine + d, 8), 1 - core, to_core)
            remote(whole.at[row], whole.at[row], sum_send.at[2], sum_recv.at[2], to)
    wait_bytes(whole.at[pl.ds(0, 15)], sum_recv.at[2])
    margin = jnp.concatenate([added(whole, 0), added(whole, 8)], axis=0) * (1.0 / CELLS)

    inverse = inverse_factor(margin)
    for x in range(XW):
        turn = dot(inverse, pencil[x], ((1,), (0,)))
        for i in range(NB):
            rotated[i, :, x, :] = turn[8 * i : 8 * i + 8]

    for db in BAND_ORDER:
        to = lax.rem(b + db, NB)
        remote(rotated.at[to], out.at[:, :, b, :], back_send, back_recv, {"band": to})
    copy = pltpu.make_async_copy(rotated.at[b], out.at[:, :, b, :], local_sem.at[1])
    copy.start()
    wait_bytes(pencil.at[:, pl.ds(0, BANDS - 1), :], pen_send)
    for stage, table in enumerate((sum_x.at[pl.ds(0, 7)], sum_y.at[pl.ds(0, 7)], whole.at[pl.ds(0, 15)])):
        wait_bytes(table, sum_send.at[stage])
    copy.wait()
    wait_bytes(own.at[pl.ds(0, NB - 1)], back_recv)
    wait_bytes(own.at[pl.ds(0, NB - 1)], back_send)


def on_device(start_bands, potential):
    f32 = jnp.float32
    dma = pltpu.SemaphoreType.DMA
    return pl.pallas_call(
        kernel,
        out_shape=jax.ShapeDtypeStruct((8, XW, YW, NZ), f32),
        in_specs=[pl.BlockSpec(memory_space=pl.ANY)] * 2,
        out_specs=pl.BlockSpec(memory_space=pl.ANY),
        scratch_shapes=[
            pltpu.VMEM((8, XW, YW, NZ), f32),
            pltpu.VMEM((XW, YW, NZ), f32),
            pltpu.VMEM((8, YW, XW, NZ), f32),
            pltpu.VMEM((YW, XW, NZ), f32),
            pltpu.VMEM((DEGREE, YW + 2 * REACH, NX, NZ), f32),
            pltpu.VMEM((YW, NX, NZ), f32),
            pltpu.VMEM((YW, NX, NZ), f32),
            pltpu.VMEM((YW, NX, NZ), f32),
            pltpu.VMEM((XW, BANDS, NZ), f32),
            pltpu.VMEM((NB, 8, XW, NZ), f32),
            pltpu.VMEM((2, 16, 128), f32),
            pltpu.VMEM((8, 16, 128), f32),
            pltpu.VMEM((8, 16, 128), f32),
            pltpu.VMEM((16, 16, 128), f32),
            pltpu.SemaphoreType.REGULAR((3,)),
            dma((3,)),
            dma,
            dma((NG,)),
            dma,
            dma,
            dma((2,)),
            dma((2, CHUNKS)),
            dma((DEGREE, 2, CHUNKS)),
            dma((DEGREE, 2, CHUNKS)),
            dma,
            dma,
            dma((3,)),
            dma((3,)),
            dma,
            dma,
        ],
        compiler_params=pltpu.CompilerParams(
            collective_id=0, has_side_effects=True, vmem_limit_bytes=24 * 1024 * 1024
        ),
    )(*[pltpu.with_memory_space_constraint(value, pltpu.HBM) for value in (start_bands, potential)])


def solution(mesh):
    in_specs = (P("band", "gx", "gy", None), P("gx", "gy", None))
    out_specs = P("band", "gx", "gy", None)
    return jax.shard_map(on_device, mesh=mesh, in_specs=in_specs, out_specs=out_specs, check_vma=False)
```

```python
import jax
import jax.numpy as jnp
from jax import lax
from jax.experimental import pallas as pl
from jax.experimental.pallas import tpu as pltpu
from jax.sharding import PartitionSpec as P

DEGREE = 4
COEFFS = (
    -5369.0 / 1800.0,
    12.0 / 7.0,
    -15.0 / 56.0,
    10.0 / 189.0,
    -1.0 / 112.0,
    2.0 / 1925.0,
    -1.0 / 16632.0,
)
LOWER_END = -0.5
CUT_LOW = 3.0
CUT_HIGH = 12.7
REACH = 6
MESH = pl.DeviceIdType.MESH
NB, NG, NY = 8, 8, 8
XW, YW, NX, NZ = 6, 8, 48, 128
BANDS = 64
CELLS = 48 * 64 * 128
CHUNKS = 3
PIECES = {2: (0, 4, 8), 3: (0, 3, 6, 8)}[CHUNKS]
GX_ORDER = (4, 5, 3, 2, 6, 7, 1)
BAND_ORDER = (4, 5, 3, 2, 6, 7, 1)
RING_ORDER = (4, 3, 5, 2, 6, 1, 7)


def filter_weights(degree):
    half_width = (CUT_HIGH - CUT_LOW) / 2.0
    middle = (CUT_HIGH + CUT_LOW) / 2.0
    sigma = half_width / (LOWER_END - middle)
    tau = 2.0 / sigma
    first = sigma / half_width
    others = []
    for index in range(degree - 1):
        sigma_new = 1.0 / (tau - sigma)
        others.append((2.0 * sigma_new / half_width, sigma * sigma_new))
        sigma = sigma_new
    return (middle, first, others)


def wait_bytes(ref, sem):
    pltpu.make_async_copy(ref, ref, sem).wait()


def dot(a, b, contract):
    return lax.dot_general(
        a,
        b,
        (contract, ((), ())),
        precision=lax.Precision.HIGHEST,
        preferred_element_type=jnp.float32,
    )


def inverse_factor(packed):
    wide = (8, 128)
    lane = lax.broadcasted_iota(jnp.int32, wide, 1)
    sub = lax.broadcasted_iota(jnp.int32, wide, 0)
    rows = []
    for t in range(8):
        part = packed[8 * (t % 4) : 8 * (t % 4) + 8]
        if t >= 4:
            part = pltpu.roll(part, 64, 1)
        unit = jnp.where(lane == sub + 8 * t, 1.0, 0.0)
        rows.append(jnp.where(lane >= 64, part, unit))
    for t in range(8):
        at = 64 + 8 * t
        row = [jnp.broadcast_to(rows[t][j : j + 1, :], wide) for j in range(8)]
        entry = {}
        for j in range(8):
            for l in range(j, 8):
                entry[j, l] = jnp.broadcast_to(rows[t][j : j + 1, at + l : at + l + 1], wide)
        column = {}
        for i in range(t + 1, 8):
            for j in range(8):
                column[i, j] = jnp.broadcast_to(rows[i][:, at + j : at + j + 1], wide)
        scaled = []
        for j in range(8):
            inverse = 1.0 / entry[j, j]
            scaled.append(row[j] * inverse)
            for l in range(j + 1, 8):
                factor = entry[j, l] * inverse
                row[l] = row[l] - factor * row[j]
                for m in range(l, 8):
                    entry[l, m] = entry[l, m] - factor * entry[j, m]
                for i in range(t + 1, 8):
                    column[i, l] = column[i, l] - column[i, j] * factor
        for i in range(t + 1, 8):
            for j in range(8):
                rows[i] = rows[i] - column[i, j] * scaled[j]
        for j in range(1, 8):
            rows[t] = jnp.where(sub == j, row[j], rows[t])
    done = []
    for t in range(8):
        pivots = jnp.sum(jnp.where(lane == sub + (8 * t + 64), rows[t], 0.0), axis=1, keepdims=True)
        done.append(rows[t] * (1.0 / jnp.sqrt(pivots)))
    return jnp.concatenate(done, axis=0)[:, :BANDS]


def kernel(
    start,
    pot,
    out,
    own,
    own_pot,
    turned,
    turned_pot,
    field,
    last,
    pots,
    acc,
    pencil,
    rotated,
    packed,
    sum_x,
    sum_y,
    whole,
    ready,
    local_sem,
    ax_send,
    ax_recv,
    pot_send,
    pot_recv,
    first_send,
    first_recv,
    halo_send,
    halo_recv,
    pen_send,
    pen_recv,
    sum_send,
    sum_recv,
    back_send,
    back_recv,
):
    b = lax.axis_index("band")
    g = lax.axis_index("gx")
    r = lax.axis_index("gy")

    def remote(src, dst, send, recv, device):
        copy = pltpu.make_async_remote_copy(
            src_ref=src, dst_ref=dst, send_sem=send, recv_sem=recv, device_id=device, device_id_type=MESH
        )
        copy.start()
        return copy

    load = pltpu.make_async_copy(start, own, local_sem.at[0])
    load.start()
    load_pot = pltpu.make_async_copy(pot, own_pot, local_sem.at[1])
    load_pot.start()

    barrier = pltpu.get_barrier_semaphore()
    core = lax.rem(b, 2)
    zhi, zlo, chip_x = b // 2, lax.rem(g, 2), g // 2
    partner = {"band": b + 1 - 2 * core}
    beside = [{"band": lax.rem(b + db, NB)} for db in (2, NB - 2)]
    greeted = beside + [partner]
    greeted += [{"gx": lax.rem(g + dg, NG)} for dg in GX_ORDER]
    greeted += [{"gy": lax.rem(r + dy, NY)} for dy in (1, NY - 1)]
    for device in greeted:
        pl.semaphore_signal(barrier, inc=1, device_id=device, device_id_type=MESH)

    load.wait()
    for i in range(NG):
        for x in range(XW):
            turned[i, :, x, :] = own[i, x]
    load_pot.wait()
    for x in range(XW):
        turned_pot[:, x, :] = own_pot[x]
    pl.semaphore_wait(barrier, len(greeted))

    slot = pl.ds(XW * g, XW)
    for dg in GX_ORDER:
        to = lax.rem(g + dg, NG)
        remote(turned.at[to], field.at[0, pl.ds(REACH, YW), slot, :], ax_send, ax_recv.at[g], {"gx": to})
    copy = pltpu.make_async_copy(turned.at[g], field.at[0, pl.ds(REACH, YW), slot, :], ax_recv.at[g])
    copy.start()

    up = {"gy": lax.rem(r + 1, NY)}
    down = {"gy": lax.rem(r + NY - 1, NY)}

    def halo(k, cols, send, recv):
        return [
            remote(
                field.at[k, pl.ds(YW, REACH), cols, :],
                field.at[k, pl.ds(0, REACH), cols, :],
                send(0),
                recv(0),
                up,
            ),
            remote(
                field.at[k, pl.ds(REACH, REACH), cols, :],
                field.at[k, pl.ds(YW + REACH, REACH), cols, :],
                send(1),
                recv(1),
                down,
            ),
        ]

    for c in range(CHUNKS):
        for source in range(PIECES[c], PIECES[c + 1]):
            cols = pl.ds(XW * source, XW)
            wait_bytes(field.at[0, pl.ds(REACH, YW), cols, :], ax_recv.at[source])
            halo(0, cols, lambda side: first_send.at[side], lambda side, c=c: first_recv.at[side, c])

    for dg in GX_ORDER:
        to = lax.rem(g + dg, NG)
        remote(turned_pot, pots.at[:, slot, :], pot_send, pot_recv, {"gx": to})
    copy_pot = pltpu.make_async_copy(turned_pot, pots.at[:, slot, :], local_sem.at[2])
    copy_pot.start()

    def tell(devices, round_):
        for device in devices:
            pl.semaphore_signal(ready.at[round_], inc=1, device_id=device, device_id_type=MESH)

    tell(beside, 0)

    middle, first, others = filter_weights(DEGREE)
    width = NX // CHUNKS
    factors = []
    for k in range(DEGREE):
        scale = first if k == 0 else others[k - 1][0]
        factors.append((scale, [-0.5 * c * scale for c in COEFFS]))

    def side_part(k, low, high):
        scale, weights = factors[k]
        for y in range(YW):
            plane = field[k, REACH + y, low:high]
            total = (3.0 * weights[0] - middle * scale) * plane
            if k:
                total = total + scale * pots[y, low:high] * plane
                total = total - others[k - 1][1] * field[k - 1, REACH + y, low:high]
            for j in range(1, REACH + 1):
                near = pltpu.roll(plane, j, 1) + pltpu.roll(plane, NZ - j, 1)
                if y - j >= 0:
                    near = near + field[k, REACH + y - j, low:high]
                if y + j < YW:
                    near = near + field[k, REACH + y + j, low:high]
                total = total + weights[j] * near
            acc[y, low:high] = total

    def x_part(k):
        weights = factors[k][1]

        def planes(i, carry):
            for y in (2 * i, 2 * i + 1):
                plane = field[k, REACH + y]
                total = acc[y]
                for j in range(1, REACH + 1):
                    total = total + weights[j] * (pltpu.roll(plane, j, 0) + pltpu.roll(plane, NX - j, 0))
                acc[y] = total
            return carry

        lax.fori_loop(0, YW // 2, planes, 0)

    band = NG * b + g

    def pass_on(targets):
        for db, to_g in [(db, to_g) for db in BAND_ORDER + (0,) for to_g in targets]:
            to_b = lax.rem(b + db, NB)
            src = last.at[to_b, pl.ds(XW * to_g, XW), :]
            dst = pencil.at[:, band, :]

            def send(src=src, dst=dst, to_b=to_b, to_g=to_g):
                remote(src, dst, pen_send, pen_recv, {"band": to_b, "gx": to_g})

            if db:
                send()
            else:
                pl.when(g != to_g)(send)

                @pl.when(g == to_g)
                def _(src=src, dst=dst):
                    pltpu.make_async_copy(src, dst, local_sem.at[0]).start()

    moves = []
    for c in range(CHUNKS):
        side_part(0, width * c, width * (c + 1))
    for k in range(DEGREE):
        scale, weights = factors[k]
        x_part(k)
        if k == 0:
            copy_pot.wait()
            wait_bytes(pots.at[:, pl.ds(0, XW * (NG - 1)), :], pot_recv)
            for y in range(YW):
                acc[y] = acc[y] + scale * pots[y] * field[0, REACH + y]
        later = []
        for c in range(CHUNKS):
            low, high = width * c, width * (c + 1)
            cols = pl.ds(low, width)
            for side in range(2):
                if k:
                    moves[c][side].wait()
                else:
                    got = pl.ds(XW * PIECES[c], XW * (PIECES[c + 1] - PIECES[c]))
                    wait_bytes(field.at[0, pl.ds((YW + REACH) * side, REACH), got, :], first_recv.at[side, c])
            for y in range(YW):
                total = acc[y, low:high]
                for j in range(1, REACH + 1):
                    if y - j < 0:
                        total = total + weights[j] * field[k, REACH + y - j, low:high]
                    if y + j >= YW:
                        total = total + weights[j] * field[k, REACH + y + j, low:high]
                if k < DEGREE - 1:
                    field[k + 1, REACH + y, low:high] = total
                else:
                    last[y, low:high] = total
            if k < DEGREE - 1:
                later.append(
                    halo(
                        k + 1,
                        cols,
                        lambda side, k=k, c=c: halo_send.at[k + 1, side, c],
                        lambda side, k=k, c=c: halo_recv.at[k + 1, side, c],
                    )
                )
                side_part(k + 1, low, high)
            else:
                if c == 0:
                    pl.semaphore_wait(ready.at[2], NG - 1)
                pass_on(range(low // XW, high // XW))
        moves = later
        if k == 0:
            pl.semaphore_wait(ready.at[0], len(beside))
            tell([partner], 1)
        if k == 1:
            pl.semaphore_wait(ready.at[1], 1)
            tell([{"gx": lax.rem(g + dg, NG)} for dg in GX_ORDER], 2)

    wait_bytes(pencil.at[:, 0, :], local_sem.at[0])
    wait_bytes(own.at[pl.ds(0, NG - 1)], ax_send)
    wait_bytes(own.at[pl.ds(0, NG - 1)], pot_send)
    for side in range(2):
        wait_bytes(field.at[0, pl.ds((YW + REACH) * side, REACH)], first_send.at[side])
    wait_bytes(pencil.at[:, pl.ds(0, BANDS - 1), :], pen_recv)

    cells = jnp.concatenate([pencil[x] for x in range(XW)], axis=1)
    twice = jnp.concatenate([cells, cells], axis=0)
    products = dot(cells, twice, ((1,), (1,)))
    lane = lax.broadcasted_iota(jnp.int32, (32, 128), 1)
    joined = jnp.where(lane < 64, products[32:], products[:32])
    packed[0] = joined[:16]
    packed[1] = joined[16:]

    piece = 2 * chip_x + core
    place = 2 * zhi + zlo

    def added(table, start_at=0):
        parts = [table[start_at + i] for i in range(8)]
        while len(parts) > 1:
            parts = [parts[i] + parts[i + 1] for i in range(0, len(parts), 2)]
        return parts[0]

    def along(index, axis, to_core):
        return {
            "band": 2 * ((1 - axis) * zhi + axis * (index // 2)) + to_core,
            "gx": (1 - axis) * g + axis * (2 * chip_x + lax.rem(index, 2)),
            "gy": (1 - axis) * index + axis * r,
        }

    for d in GX_ORDER:
        other = lax.rem(piece + d, 8)
        to_core = lax.rem(other, 2)
        remote(
            packed.at[to_core],
            sum_x.at[piece],
            sum_send.at[0],
            sum_recv.at[0],
            {"band": 2 * zhi + to_core, "gx": 2 * (other // 2) + zlo},
        )
    sum_x[piece] = packed[core]
    wait_bytes(sum_x.at[pl.ds(0, 7)], sum_recv.at[0])

    mine = (1 - core) * r + core * place
    sum_y[mine] = added(sum_x)
    for d in RING_ORDER:
        to = along(lax.rem(mine + d, 8), core, core)
        remote(sum_y.at[mine], sum_y.at[mine], sum_send.at[1], sum_recv.at[1], to)
    wait_bytes(sum_y.at[pl.ds(0, 7)], sum_recv.at[1])

    mine = (1 - core) * place + core * r
    row = 8 * core + mine
    whole[row] = added(sum_y)
    for d in RING_ORDER + (0,):
        for to_core in (1 - core, core)[: 2 if d else 1]:
            to = along(lax.rem(mine + d, 8), 1 - core, to_core)
            remote(whole.at[row], whole.at[row], sum_send.at[2], sum_recv.at[2], to)
    wait_bytes(whole.at[pl.ds(0, 15)], sum_recv.at[2])
    margin = jnp.concatenate([added(whole, 0), added(whole, 8)], axis=0) * (1.0 / CELLS)

    inverse = inverse_factor(margin)
    copies = []
    for part in range(2):
        for x in range(3):
            turn = dot(inverse, pencil[3 * part + x], ((1,), (0,)))
            for i in range(NB):
                rotated[part, i, :, x, :] = turn[8 * i : 8 * i + 8]
        there = pl.ds(3 * part, 3)
        for db in BAND_ORDER:
            to = lax.rem(b + db, NB)
            remote(rotated.at[part, to], out.at[:, there, b, :], back_send, back_recv, {"band": to})
        copy = pltpu.make_async_copy(rotated.at[part, b], out.at[:, there, b, :], local_sem.at[1 + part])
        copy.start()
        copies.append(copy)
    wait_bytes(pencil.at[:, pl.ds(0, BANDS - 1), :], pen_send)
    for stage, table in enumerate((sum_x.at[pl.ds(0, 7)], sum_y.at[pl.ds(0, 7)], whole.at[pl.ds(0, 15)])):
        wait_bytes(table, sum_send.at[stage])
    for copy in copies:
        copy.wait()
    wait_bytes(own.at[pl.ds(0, NB - 1)], back_recv)
    wait_bytes(own.at[pl.ds(0, NB - 1)], back_send)


def on_device(start_bands, potential):
    f32 = jnp.float32
    dma = pltpu.SemaphoreType.DMA
    return pl.pallas_call(
        kernel,
        out_shape=jax.ShapeDtypeStruct((8, XW, YW, NZ), f32),
        in_specs=[pl.BlockSpec(memory_space=pl.ANY)] * 2,
        out_specs=pl.BlockSpec(memory_space=pl.ANY),
        scratch_shapes=[
            pltpu.VMEM((8, XW, YW, NZ), f32),
            pltpu.VMEM((XW, YW, NZ), f32),
            pltpu.VMEM((8, YW, XW, NZ), f32),
            pltpu.VMEM((YW, XW, NZ), f32),
            pltpu.VMEM((DEGREE, YW + 2 * REACH, NX, NZ), f32),
            pltpu.VMEM((YW, NX, NZ), f32),
            pltpu.VMEM((YW, NX, NZ), f32),
            pltpu.VMEM((YW, NX, NZ), f32),
            pltpu.VMEM((XW, BANDS, NZ), f32),
            pltpu.VMEM((2, NB, 8, 3, NZ), f32),
            pltpu.VMEM((2, 16, 128), f32),
            pltpu.VMEM((8, 16, 128), f32),
            pltpu.VMEM((8, 16, 128), f32),
            pltpu.VMEM((16, 16, 128), f32),
            pltpu.SemaphoreType.REGULAR((3,)),
            dma((3,)),
            dma,
            dma((NG,)),
            dma,
            dma,
            dma((2,)),
            dma((2, CHUNKS)),
            dma((DEGREE, 2, CHUNKS)),
            dma((DEGREE, 2, CHUNKS)),
            dma,
            dma,
            dma((3,)),
            dma((3,)),
            dma,
            dma,
        ],
        compiler_params=pltpu.CompilerParams(
            collective_id=0, has_side_effects=True, vmem_limit_bytes=24 * 1024 * 1024
        ),
    )(*[pltpu.with_memory_space_constraint(value, pltpu.HBM) for value in (start_bands, potential)])


def solution(mesh):
    in_specs = (P("band", "gx", "gy", None), P("gx", "gy", None))
    out_specs = P("band", "gx", "gy", None)
    return jax.shard_map(on_device, mesh=mesh, in_specs=in_specs, out_specs=out_specs, check_vma=False)
```
